32 devices in a mesh: row: 8 (over y, x, core), col: 4 (over z).
Axes of the slice: x: 2, y: 2, z: 4, core: 2. Of those that a mesh axis runs over, the one named last changes fastest.
Arguments:
- panel_index: int32 [16], replicated, may hold values 0 or 1
- row_sites: int32 [2048], replicated, may hold values from 0 to 2047, each once
- site_coords: float32 [2, 2048], replicated, may hold values from 0 to 1
- new_coords: float32 [2, 2048], P(None, 'col'), may hold values from 0 to 1
- factor_earlier: bfloat16 [2048, 16384], P(None, 'row'), may hold values from -0.0625 to 0.0625
- solved_earlier: bfloat16 [16384, 2048], P('row', 'col'), may hold values from -6 to 6
- panel_inverse: bfloat16 [2048, 2048], P('row'), as said below
- trailing_rhs: float32 [2048, 2048], P('row', 'col'), may hold values from -6 to 6
- factor_trailing: bfloat16 [2048, 2048], P('row'), may hold values from -0.125 to 0.125
- prior_cov: float32 [2048, 2048], P('row', 'col'), may hold values from -4 to 4
Outputs:
- solved_panel: bfloat16 [2048, 2048], P('row', 'col')
- trailing_out: float32 [2048, 2048], P('row', 'col')
- cond_cov: float32 [2048, 2048], P('row', 'col')
The draws below stay inside these ranges and needn't reach their ends.
Inputs may be any that keep to these rules, and one draw needn't show every extreme that they name: `row_sites`: each site 0 to 2047 appears once. `panel_inverse`: lower triangular, with diagonal entries between 0.5 and 1.5.
All inputs are finite; a program needn't handle non-finite values.
Results may differ from the reference program's by a relative error of at most 0.0049.
Values may be sent and summed in bfloat16 or wider, within the bound.
No kernel may reach another device: no remote copies, remote signals or barrier semaphores. Data moves between devices by JAX's collectives and lax.ppermute only.
A program may use at most 64 MiB of HBM per device.

```python
import math
import jax
import jax.numpy as jnp
from jax import lax

P_SIZE = 2048
PANELS = 16
M = 2048
E = 16384
TR = 2048


def draw_panel_inverse(key, part):
    first_key, second_key = jax.random.split(jax.random.fold_in(key, 17))
    row_ids = jnp.arange(P_SIZE, dtype=jnp.int32)[:, None]
    col_ids = jnp.arange(P_SIZE, dtype=jnp.int32)[None, :]
    below = jax.random.normal(first_key, (P_SIZE, P_SIZE), jnp.float32) * P_SIZE ** (-0.5)
    diagonal = jax.random.uniform(second_key, (P_SIZE, 1), jnp.float32, 0.5, 1.5)
    lower = jnp.where(col_ids < row_ids, below, 0.0) + jnp.where(col_ids == row_ids, diagonal, 0.0)
    return lower.astype(jnp.bfloat16)


def with_ends(result, rng, smallest, top_value):
    longest = result.shape.index(max(result.shape))
    spots = []
    for shift in (0, 1):
        where = [jax.random.randint(jax.random.fold_in(rng, axis), (), 0, length) for axis, length in enumerate(result.shape)]
        where[longest] = (where[longest] + shift) % result.shape[longest]
        spots.append(tuple(where))
    return result.at[spots[0]].set(smallest).at[spots[1]].set(top_value)


def with_spikes(drawn, own_key, source, target, blocks, factor):
    owner, partner = [(jnp.arange(drawn.shape[position]) // (drawn.shape[position] // blocks)).reshape([-1 if axis == position else 1 for axis in range(drawn.ndim)]) for position in (source, target)]
    chosen = jax.random.permutation(own_key, blocks)[partner]
    strong = (owner == chosen) | (owner == (partner + blocks // 2) % blocks)
    return jnp.where(strong, factor * drawn, drawn)


def steps_of(own_key, extent, cuts, least, top_value):
    gain, own = 1.0, jax.random.fold_in(own_key, 6)
    for axis_at, blocks in cuts:
        steps = jnp.exp(jax.random.uniform(jax.random.fold_in(own, axis_at), (blocks,), jnp.float32, least / len(cuts), top_value / len(cuts)))
        gain = gain * jnp.repeat(steps, extent[axis_at] // blocks).reshape([-1 if axis == axis_at else 1 for axis in range(len(extent))])
    return gain


def centred(rng, dims, spread, bound, cuts=(), kind=jnp.bfloat16):
    entries = spread * jax.random.normal(rng, dims, jnp.float32)
    if cuts:
        entries = entries * steps_of(rng, dims, cuts, -0.22, 0.18)
    return jnp.clip(entries, -bound, bound).astype(kind)


def heavy_noise(rng, extent, width, bound, pieces, heavy, kind=jnp.bfloat16):
    entries = width * jax.random.normal(rng, extent, jnp.float32)
    if pieces:
        entries = entries * steps_of(rng, extent, pieces, -0.22, 0.18)
    return jnp.clip(with_spikes(entries, jax.random.fold_in(rng, 3), *heavy), -bound, bound).astype(kind)


def setup_inputs(seed: int = 0) -> dict:
    key_list = jax.random.split(jax.random.key(seed), 11)
    return {
        "panel_index": with_ends((jax.random.randint(key_list[0], (PANELS,), 0, 2) < 1).astype(jnp.int32), jax.random.fold_in(key_list[0], 1), 0, 1),
        "row_sites": jax.random.permutation(key_list[1], P_SIZE).astype(jnp.int32),
        "site_coords": jnp.clip(jax.random.uniform(key_list[2], (2, P_SIZE), jnp.float32, 0.0, 1.0), 0.0, 1.0),
        "new_coords": jnp.clip(1.0 * jax.random.uniform(key_list[3], (2, M), jnp.float32) ** steps_of(key_list[3], (2, M), ((1, 4),), -0.2, 0.2), 0.0, 1.0),
        "factor_earlier": heavy_noise(key_list[4], (P_SIZE, E), E ** -0.5, 0.0625, ((1, 8),), (1, 0, 8, 2.0)),
        "solved_earlier": centred(key_list[5], (E, M), 1.0, 6.0, ((0, 8), (1, 4))),
        "panel_inverse": draw_panel_inverse(jax.random.fold_in(key_list[10], 71), 0),
        "trailing_rhs": centred(key_list[7], (TR, M), 1.0, 6.0, ((0, 8), (1, 4)), jnp.float32),
        "factor_trailing": centred(key_list[8], (TR, P_SIZE), P_SIZE ** -0.5, 0.125, ((0, 8),)),
        "prior_cov": centred(key_list[9], (M, M), 0.5, 4.0, ((0, 8), (1, 4)), jnp.float32),
    }


length_scale = 0.5

def matern(distance):
    scaled = distance * (math.sqrt(3.0) / length_scale)
    return (1.0 + scaled) * jnp.exp(-scaled)

def reference(panel_index, row_sites, site_coords, new_coords, factor_earlier, solved_earlier, panel_inverse, trailing_rhs, factor_trailing, prior_cov):
    rows_xy = jnp.take(site_coords, row_sites, axis=1)
    delta_x = rows_xy[0][:, None] - new_coords[0][None, :]
    delta_y = rows_xy[1][:, None] - new_coords[1][None, :]
    cross_cov = matern(jnp.sqrt(delta_x * delta_x + delta_y * delta_y))
    global_rows = jnp.arange(E, dtype=jnp.int32)
    wanted = jnp.take(panel_index, global_rows % PANELS) > 0
    masked = jnp.where(wanted[:, None], solved_earlier, jnp.zeros_like(solved_earlier))
    partial_value = jnp.dot(factor_earlier, masked, preferred_element_type=jnp.float32)
    right_side = (cross_cov - partial_value).astype(jnp.bfloat16)
    solved = jnp.dot(panel_inverse, right_side, preferred_element_type=jnp.float32).astype(jnp.bfloat16)
    trailing_out = trailing_rhs - jnp.dot(factor_trailing, solved, preferred_element_type=jnp.float32)
    gram_sum = lax.dot_general(solved, solved, (((0,), (0,)), ((), ())), preferred_element_type=jnp.float32)
    cond_cov = prior_cov - gram_sum * (1.0 / P_SIZE)
    return (solved, trailing_out, cond_cov)
```

```python
import math

import jax
import jax.numpy as jnp
from jax import lax
from jax.sharding import PartitionSpec as P

length_scale = 0.5
CORES = 2


def matern(distance):
    scaled = distance * (math.sqrt(3.0) / length_scale)
    return (1.0 + scaled) * jnp.exp(-scaled)


def cross_tile(site_coords, chosen_sites, new_coords):
    rows_xy = jnp.take(site_coords, chosen_sites, axis=1)
    delta_x = rows_xy[0][:, None] - new_coords[0][None, :]
    delta_y = rows_xy[1][:, None] - new_coords[1][None, :]
    return matern(jnp.sqrt(delta_x * delta_x + delta_y * delta_y))


def product(first, second):
    return jnp.dot(first, second, preferred_element_type=jnp.float32)


def transpose_product(first_rows, second_rows):
    return lax.dot_general(
        first_rows, second_rows, (((0,), (0,)), ((), ())), preferred_element_type=jnp.float32
    )


def make_per_device(row_count, col_count):
    chips = row_count // CORES

    def to_partner(value):
        return lax.ppermute(value, "row", [(r, r ^ 1) for r in range(row_count)])

    def to_chip(value, step):
        return lax.ppermute(value, "row", [(r, r ^ (CORES * step)) for r in range(row_count)])

    def around_col(value, hop):
        pairs = []
        for r in range(row_count):
            root = r // CORES
            begin = (root + hop - 1) % col_count
            end = (root + hop) % col_count
            pairs.append((r * col_count + begin, r * col_count + end))
        return lax.ppermute(value, ("row", "col"), pairs)

    def per_device(
        panel_index,
        row_sites,
        site_coords,
        new_coords,
        factor_earlier,
        solved_earlier,
        panel_inverse,
        trailing_rhs,
        factor_trailing,
        prior_cov,
    ):
        row_place = lax.axis_index("row")
        col_place = lax.axis_index("col")
        core = row_place % CORES
        chip = row_place // CORES
        local_rows = panel_inverse.shape[0]
        panel_rows = panel_inverse.shape[1]
        earlier_rows = solved_earlier.shape[0]
        new_cols = new_coords.shape[1]
        cov_rows = prior_cov.shape[0]
        class_count = panel_index.shape[0]
        half = new_cols // CORES
        chip_rows = local_rows * CORES

        if earlier_rows % class_count == 0:
            flags = jnp.tile(panel_index, earlier_rows // class_count)
        else:
            global_rows = row_place * earlier_rows + jnp.arange(earlier_rows, dtype=jnp.int32)
            flags = jnp.take(panel_index, global_rows % class_count)
        flags = flags.astype(jnp.bfloat16)[:, None]
        other_cols = lax.dynamic_slice_in_dim(solved_earlier, (1 - core) * half, half, 1) * flags
        own_cols = lax.dynamic_slice_in_dim(solved_earlier, core * half, half, 1) * flags

        inverse_other = to_partner(panel_inverse)
        partial_other = product(factor_earlier, other_cols).astype(jnp.bfloat16)
        partial_got = to_partner(partial_other)
        partial_own = product(factor_earlier, own_cols)
        chip_sum = partial_own + partial_got.astype(jnp.float32)

        def chunk(step):
            return lax.dynamic_slice_in_dim(chip_sum, (chip ^ step) * chip_rows, chip_rows, 0)

        arrived = [to_chip(chunk(step).astype(jnp.bfloat16), step) for step in range(1, chips)]

        def relative(value):
            return jnp.concatenate(
                [
                    lax.dynamic_slice_in_dim(value, (chip ^ step) * chip_rows, chip_rows, 1)
                    for step in range(chips)
                ],
                axis=1,
            )

        first_rows = jnp.where(core == 0, panel_inverse, inverse_other)
        second_rows = jnp.where(core == 0, inverse_other, panel_inverse)
        inverse_chip = relative(jnp.concatenate([first_rows, second_rows], axis=0))
        trailing_factor = relative(factor_trailing)

        own_sites = lax.dynamic_slice_in_dim(row_sites, chip * chip_rows, chip_rows, 0)
        half_coords = lax.dynamic_slice_in_dim(new_coords, core * half, half, 1)
        cross_cov = cross_tile(site_coords, own_sites, half_coords)

        total = chunk(0)
        for piece in arrived:
            total = total + piece.astype(jnp.float32)
        right_own = (cross_cov - total).astype(jnp.bfloat16)
        right_parts = [right_own] + [to_chip(right_own, step) for step in range(1, chips)]
        solved_own = product(inverse_chip, jnp.concatenate(right_parts, axis=0)).astype(
            jnp.bfloat16
        )

        away = lax.dynamic_slice_in_dim(solved_own, (1 - core) * local_rows, local_rows, 0)
        home = lax.dynamic_slice_in_dim(solved_own, core * local_rows, local_rows, 0)
        back = to_partner(away)

        def both(mine, theirs):
            return jnp.concatenate(
                [jnp.where(core == 0, mine, theirs), jnp.where(core == 0, theirs, mine)], axis=1
            )

        solved = both(home, back)

        solved_parts = [solved_own] + [to_chip(solved_own, step) for step in range(1, chips)]
        mine = jnp.concatenate(solved_parts, axis=0)
        theirs = to_partner(mine)
        gathered = both(mine, theirs)
        trailing_out = trailing_rhs - product(trailing_factor, gathered)

        if new_cols == CORES * cov_rows and chips == col_count:
            hops_away = (col_place - chip) % col_count
            blocks = []
            for part in solved_parts:
                moving = part
                block = part
                for hop in range(1, col_count):
                    moving = around_col(moving, hop)
                    block = jnp.where(hops_away == hop, moving, block)
                blocks.append(block)
            column_block = jnp.concatenate(blocks, axis=0)
        else:
            source = row_place * cov_rows // new_cols
            offset = row_place * cov_rows - source * new_cols
            column_block = lax.dynamic_slice_in_dim(gathered, offset, cov_rows, 1)
            column_block = jnp.where(col_place == source, column_block, jnp.zeros_like(column_block))
            column_block = lax.psum(column_block, "col")
        cond_cov = prior_cov - transpose_product(column_block, gathered) * (1.0 / panel_rows)
        return (solved, trailing_out, cond_cov)

    return per_device


def solution(mesh):
    return jax.shard_map(
        make_per_device(mesh.shape["row"], mesh.shape["col"]),
        mesh=mesh,
        in_specs=(
            P(),
            P(),
            P(),
            P(None, "col"),
            P(None, "row"),
            P("row", "col"),
            P("row", None),
            P("row", "col"),
            P("row", None),
            P("row", "col"),
        ),
        out_specs=(P("row", "col"), P("row", "col"), P("row", "col")),
        check_vma=False,
    )
```

```python
import functools
import math

import jax
import jax.numpy as jnp
from jax import lax
from jax.experimental import pallas as pl
from jax.experimental.pallas import tpu as pltpu
from jax.sharding import PartitionSpec as P


length_scale = 0.5
CORES = 2
CHUNKS = 2


def matern(distance):
    scaled = distance * (math.sqrt(3.0) / length_scale)
    return (1.0 + scaled) * jnp.exp(-scaled)


def product(first, second):
    return jnp.dot(first, second, preferred_element_type=jnp.float32)


def transpose_product(first_rows, second_rows):
    return lax.dot_general(
        first_rows, second_rows, (((0,), (0,)), ((), ())), preferred_element_type=jnp.float32
    )


def after(value, *others):
    return lax.optimization_barrier((value, *others))[0]


def in_vmem(value):
    return pltpu.with_memory_space_constraint(value, pltpu.VMEM)


def in_hbm(value):
    return pltpu.with_memory_space_constraint(value, pltpu.HBM)


def keep_wanted(flags, value):
    count = flags.shape[0]
    depth, width = value.shape
    class_of = lax.broadcasted_iota(jnp.int32, (count, width), 0)
    keep = jnp.zeros((count, width), jnp.int32)
    for place in range(count):
        keep = jnp.where(class_of == place, flags[place], keep)
    keep = keep.astype(jnp.float32).astype(value.dtype)
    return (value.reshape(depth // count, count, width) * keep[None]).reshape(depth, width)


def sums_kernel(places, flags, factor, solved, *refs, chips):
    outs = refs[: 2 * CHUNKS]
    masked, solved_in, factor_in, flags_in, sems, solved_sem, flags_sem = refs[2 * CHUNKS :]
    width = outs[0].shape[1]
    half = width * CHUNKS
    block = factor.shape[0] // chips
    flags_copy = pltpu.make_async_copy(flags, flags_in, flags_sem)
    solved_copy = pltpu.make_async_copy(solved, solved_in, solved_sem)
    blocks = [
        pltpu.make_async_copy(
            factor.at[pl.ds(pl.multiple_of((places[0] ^ step) * block, block), block), :],
            factor_in.at[step],
            sems.at[step],
        )
        for step in range(chips)
    ]
    flags_copy.start()
    solved_copy.start()
    blocks[0].start()
    flags_copy.wait()
    solved_copy.wait()
    for copy in blocks[1:]:
        copy.start()

    for core in range(CORES):

        @pl.when(places[1] == core)
        def _():
            for chunk in range(CHUNKS):
                for side, at in ((0, 1 - core), (1, core)):
                    start = at * half + chunk * width
                    column = (chunk * CORES + side) * width
                    masked[:, column : column + width] = keep_wanted(
                        flags_in, solved_in[:, start : start + width]
                    )

    for step in range(chips):
        blocks[step].wait()
        rows = slice(step * block, (step + 1) * block)
        for chunk in range(CHUNKS):
            column = chunk * CORES * width
            sums = jnp.dot(
                factor_in[step],
                masked[:, column : column + CORES * width],
                preferred_element_type=jnp.float32,
            )
            outs[2 * chunk][rows, :] = sums[:, :width].astype(jnp.bfloat16)
            outs[2 * chunk + 1][rows, :] = sums[:, width:]


def partial_sums(places, flags, factor, solved, width, chips):
    rows, depth = factor.shape
    far = pl.BlockSpec(memory_space=pltpu.HBM)
    outs = [
        pltpu.VMEM((rows, width), jnp.bfloat16),
        pltpu.VMEM((rows, width), jnp.float32),
    ] * CHUNKS
    return pl.pallas_call(
        functools.partial(sums_kernel, chips=chips),
        in_specs=[pl.BlockSpec(memory_space=pltpu.SMEM), far, far, far],
        out_specs=[pl.BlockSpec(memory_space=pltpu.VMEM)] * len(outs),
        out_shape=outs,
        scratch_shapes=[
            pltpu.VMEM(solved.shape, solved.dtype),
            pltpu.VMEM(solved.shape, solved.dtype),
            pltpu.VMEM((chips, rows // chips, depth), factor.dtype),
            pltpu.SMEM(flags.shape, flags.dtype),
            pltpu.SemaphoreType.DMA((chips,)),
            pltpu.SemaphoreType.DMA,
            pltpu.SemaphoreType.DMA,
        ],
        compiler_params=pltpu.CompilerParams(vmem_limit_bytes=28 * 2**20),
        name="partial_sums",
    )(places, in_hbm(flags), in_hbm(factor), in_hbm(solved))


def cross_kernel(places, sites, coords, fresh, out):
    count = coords.shape[1]
    rows, columns = out.shape
    chosen = sites[:, pl.ds(pl.multiple_of(places[0] * rows, rows), rows)]
    picked = lax.broadcasted_iota(jnp.int32, (count, rows), 0) == chosen
    picked = jnp.where(picked, 1.0, 0.0).astype(jnp.bfloat16)
    rest = coords[...]
    total = jnp.zeros((coords.shape[0], rows), jnp.float32)
    for _ in range(3):
        part = rest.astype(jnp.bfloat16)
        rest = rest - part.astype(jnp.float32)
        total = total + jnp.dot(part, picked, preferred_element_type=jnp.float32)
    here = jnp.transpose(total)
    start = pl.multiple_of(places[1] * columns, columns)
    there = fresh[:, pl.ds(start, columns)]
    delta_x = here[:, 0:1] - there[0:1, :]
    delta_y = here[:, 1:2] - there[1:2, :]
    out[...] = matern(jnp.sqrt(delta_x * delta_x + delta_y * delta_y))


def cross_tile(places, row_sites, site_coords, new_coords, rows, columns):
    pad = [(0, 8 - site_coords.shape[0]), (0, 0)]
    return pl.pallas_call(
        cross_kernel,
        in_specs=[pl.BlockSpec(memory_space=pltpu.SMEM)]
        + [pl.BlockSpec(memory_space=pltpu.VMEM)] * 3,
        out_specs=pl.BlockSpec(memory_space=pltpu.VMEM),
        out_shape=jax.ShapeDtypeStruct((rows, columns), jnp.float32),
        compiler_params=pltpu.CompilerParams(vmem_limit_bytes=16 * 2**20),
        name="cross_tile",
    )(places, row_sites[None, :], jnp.pad(site_coords, pad), new_coords)


def add_kernel(own, got, *refs):
    outs, (got_in, sem) = refs[:-2], refs[-2:]
    block = outs[0].shape[0]
    copy = pltpu.make_async_copy(got, got_in, sem)
    copy.start()
    copy.wait()
    for at, out in enumerate(outs):
        rows = slice((at + 1) * block, (at + 2) * block)
        out[...] = (own[rows, :] + got_in[rows, :].astype(jnp.float32)).astype(out.dtype)


def add_partner(own, got, chips):
    rows, width = own.shape
    near = pl.BlockSpec(memory_space=pltpu.VMEM)
    return pl.pallas_call(
        add_kernel,
        in_specs=[near, pl.BlockSpec(memory_space=pltpu.HBM)],
        out_specs=[near] * (chips - 1),
        out_shape=[pltpu.VMEM((rows // chips, width), got.dtype)] * (chips - 1),
        scratch_shapes=[pltpu.VMEM((rows, width), got.dtype), pltpu.SemaphoreType.DMA],
        compiler_params=pltpu.CompilerParams(vmem_limit_bytes=16 * 2**20),
        name="add_partner",
    )(in_vmem(own), in_hbm(got))


def make_per_device(row_count, col_count):
    chips = row_count // CORES

    steps = sorted(range(1, chips), key=lambda step: -step.bit_count())
    col_steps = list(range(col_count - 1, 0, -1))

    def to_partner(value):
        return lax.ppermute(value, "row", [(r, r ^ 1) for r in range(row_count)])

    def to_chips(value):
        got = {}
        for step in steps:
            got[step] = lax.ppermute(
                value(step), "row", [(r, r ^ (CORES * step)) for r in range(row_count)]
            )
        return got

    def to_cols(value):
        got = {0: value}
        for step in col_steps:
            got[step] = lax.ppermute(value, "col", [(c, c ^ step) for c in range(col_count)])
        return got

    def per_device(
        panel_index,
        row_sites,
        site_coords,
        new_coords,
        factor_earlier,
        solved_earlier,
        panel_inverse,
        trailing_rhs,
        factor_trailing,
        prior_cov,
    ):
        row_place = lax.axis_index("row")
        col_place = lax.axis_index("col")
        core = row_place % CORES
        chip = row_place // CORES
        local_rows = panel_inverse.shape[0]
        panel_rows = panel_inverse.shape[1]
        earlier_rows = solved_earlier.shape[0]
        new_cols = new_coords.shape[1]
        cov_rows = prior_cov.shape[0]
        class_count = panel_index.shape[0]
        half = new_cols // CORES
        chip_rows = local_rows * CORES

        width = half // CHUNKS
        spans = [slice(q * width, (q + 1) * width) for q in range(CHUNKS)]
        ring = new_cols == CORES * cov_rows and chips == col_count

        if earlier_rows % class_count:
            panel_index = jnp.roll(panel_index, -(row_place * earlier_rows))

        def rows_of(value, step):
            return value[step * chip_rows : (step + 1) * chip_rows]

        places = jnp.stack([chip, core]).astype(jnp.int32)
        sums = partial_sums(
            places, panel_index, factor_earlier, solved_earlier, width, chips
        )
        sent = [to_partner(sums[2 * q]) for q in range(CHUNKS)]
        kept = [sums[2 * q + 1] for q in range(CHUNKS)]
        outgoing = []
        for q in range(CHUNKS):
            if q:
                sent[q] = after(sent[q], outgoing[-1][1])
            added = add_partner(kept[q], sent[q], chips)
            outgoing.append(dict(enumerate(added, start=1)))
        arrived = [to_chips(outgoing[q].get) for q in range(CHUNKS)]

        def relative(value):
            return jnp.concatenate(
                [
                    lax.dynamic_slice_in_dim(value, (chip ^ step) * chip_rows, chip_rows, 1)
                    for step in range(chips)
                ],
                axis=1,
            )

        row_sites, site_coords, new_coords, _ = lax.optimization_barrier(
            (row_sites, site_coords, new_coords, kept[-1])
        )
        cross_cov = cross_tile(places, row_sites, site_coords, new_coords, chip_rows, half)

        inverse_other = to_partner(panel_inverse)
        first_rows = jnp.where(core == 0, panel_inverse, inverse_other)
        second_rows = jnp.where(core == 0, inverse_other, panel_inverse)
        inverse_chip = relative(after(jnp.concatenate([first_rows, second_rows], axis=0), cross_cov))

        right_owns = []
        rights = []
        for q, span in enumerate(spans):
            total = rows_of(kept[q], 0) + rows_of(sent[q], 0)
            for step in steps:
                piece = arrived[q][step]
                if q:
                    piece = after(piece, right_owns[-1])
                total = total + piece.astype(jnp.float32)
            right_own = (cross_cov[:, span] - total).astype(jnp.bfloat16)
            right_owns.append(right_own)
            rights.append(to_chips(lambda step: right_own))

        trailing_factor = relative(after(factor_trailing, *right_owns))

        solved_chunks = []
        mine = []
        columns = []
        for q in range(CHUNKS):
            right = jnp.concatenate(
                [right_owns[q]] + [rights[q][step] for step in range(1, chips)], axis=0
            )
            solved_own = product(inverse_chip, right).astype(jnp.bfloat16)
            solved_chunks.append(solved_own)
            got = to_chips(lambda step: solved_own)
            mine.append(
                jnp.concatenate([solved_own] + [got[step] for step in range(1, chips)], axis=0)
            )
            if ring:
                blocks = to_cols(solved_own)

                def of_chip(step):
                    apart = (chip ^ step) ^ col_place
                    value = blocks[0]
                    for other in col_steps:
                        value = jnp.where(apart == other, blocks[other], value)
                    return value

                spread = to_chips(of_chip)
                columns.append(
                    jnp.concatenate(
                        [of_chip(0)] + [spread[step] for step in range(1, chips)], axis=0
                    )
                )
        theirs = [to_partner(mine[q]) for q in range(CHUNKS)]

        def both(own, others):
            own = jnp.concatenate(own, axis=1)
            others = jnp.concatenate(others, axis=1)
            return jnp.concatenate(
                [jnp.where(core == 0, own, others), jnp.where(core == 0, others, own)], axis=1
            )

        solved_own = jnp.concatenate(solved_chunks, axis=1)
        away = lax.dynamic_slice_in_dim(solved_own, (1 - core) * local_rows, local_rows, 0)
        home = lax.dynamic_slice_in_dim(solved_own, core * local_rows, local_rows, 0)
        solved = both([home], [to_partner(away)])

        gathered = both(mine, theirs)
        trailing_out = trailing_rhs - product(trailing_factor, gathered)
        if ring:
            column_block = jnp.concatenate(columns, axis=1)
        else:
            source = row_place * cov_rows // new_cols
            offset = row_place * cov_rows - source * new_cols
            column_block = lax.dynamic_slice_in_dim(gathered, offset, cov_rows, 1)
            column_block = jnp.where(col_place == source, column_block, jnp.zeros_like(column_block))
            column_block = lax.psum(column_block, "col")
        cond_cov = prior_cov - transpose_product(column_block, gathered) * (1.0 / panel_rows)
        return (solved, trailing_out, cond_cov)

    return per_device


def solution(mesh):
    row_count = mesh.shape["row"]
    col_count = mesh.shape["col"]
    return jax.shard_map(
        make_per_device(row_count, col_count),
        mesh=mesh,
        in_specs=(
            P(),
            P(),
            P(),
            P(None, "col"),
            P(None, "row"),
            P("row", "col"),
            P("row", None),
            P("row", "col"),
            P("row", None),
            P("row", "col"),
        ),
        out_specs=(P("row", "col"), P("row", "col"), P("row", "col")),
        check_vma=False,
    )
```
